128 devices in a mesh: tbit: 4 (over x), box: 32 (over y, z, core).
Axes of the slice: x: 4, y: 4, z: 4, core: 2. Of those that a mesh axis runs over, the one named last changes fastest.
Arguments:
- coeffs: float32 [64, 64, 4, 64, 256], P(None, 'box', 'tbit'), may hold values from -6 to 6
- skeleton_first: int32 [64, 64, 4, 64], P(None, 'box'), may hold values from 0 to 4095, as said below
- skeleton_second: int32 [64, 64, 4, 64], P(None, 'box'), may hold values from 0 to 8191, as said below
- skeleton_third: int32 [64, 64, 4, 64], P(None, 'box'), may hold values from 0 to 16383, as said below
- checks_first: int32 [128, 64], replicated, may hold values from 0 to 8191, as said below
- checks_second: int32 [256, 64], replicated, may hold values from 0 to 4095, as said below
- checks_third: int32 [512, 64], replicated, may hold values from 0 to 2047, as said below
- ranks_first: int32 [64, 64, 4], P(None, 'box', 'tbit'), may hold values from 32 to 64
- ranks_second: int32 [64, 64, 4], P(None, 'box', 'tbit'), may hold values from 32 to 64
- ranks_third: int32 [64, 4, 2, 32], replicated, may hold values from 32 to 64
- interpolants: float32 [3, 64, 64], replicated, may hold values from -0.09375 to 0.09375
- owners: int32 [4, 64], replicated, may hold values from 0 to 31, as said below
Outputs:
- switched: float32 [4, 32, 2, 4, 32, 64, 256], P('tbit', 'box')
The draws below stay inside these ranges and needn't reach their ends.
Inputs may be any that keep to these rules, and one draw needn't show every extreme that they name: `skeleton_first`: entry r lies in the r-th of 64 equal parts of its source box of 4096 points. `skeleton_second`: entry r lies in the r-th of 64 equal parts of its source box of 8192 points. `skeleton_third`: entry r lies in the r-th of 64 equal parts of its source box of 16384 points. `checks_first`: entry r lies in the r-th of 64 equal parts of its target box. `checks_second`: entry r lies in the r-th of 64 equal parts of its target box. `checks_third`: entry r lies in the r-th of 64 equal parts of its target box. `owners`: in each row no box index is named more than 4 times, and some index exactly 4 times.
All inputs are finite; a program needn't handle non-finite values.
Results may differ from the reference program's by a relative error of at most 0.0003.
Values sent between devices are 32-bit elements; how exact they have to be, the bound alone decides.
A program may use at most 128 MiB of HBM per device.

```python
import math
import jax
import jax.numpy as jnp
from jax import lax

R = 64
NPTS = 1048576
A0 = 64
NV = 256
NB = 32
NH = 64
CAP = 4


def box_offsets(key, shape, box_points):
    step_size = box_points // R
    spread = jnp.arange(R, dtype=jnp.int32) * step_size
    return spread + jax.random.randint(key, shape, 0, step_size, dtype=jnp.int32)


def draw_skeleton_first(key, part):
    return box_offsets(jax.random.fold_in(key, 11), (A0, NH, 4, R), NPTS // (4 * NH))


def draw_skeleton_second(key, part):
    return box_offsets(jax.random.fold_in(key, 12), (A0, NH, 4, R), NPTS // (2 * NH))


def draw_skeleton_third(key, part):
    return box_offsets(jax.random.fold_in(key, 13), (A0, NH, 4, R), NPTS // NH)


def draw_checks_first(key, part):
    return box_offsets(jax.random.fold_in(key, 21), (2 * A0, R), NPTS // (2 * A0))


def draw_checks_second(key, part):
    return box_offsets(jax.random.fold_in(key, 22), (4 * A0, R), NPTS // (4 * A0))


def draw_checks_third(key, part):
    return box_offsets(jax.random.fold_in(key, 23), (8 * A0, R), NPTS // (8 * A0))


def draw_owners(key, part):
    box_total = NH // 2

    def one_row(row_key):
        first_key, second_key, third_key = jax.random.split(row_key, 3)
        busiest = jax.random.randint(first_key, (), 0, box_total, dtype=jnp.int32)
        others = jax.random.permutation(second_key, (box_total - 1) * CAP)[:A0 - CAP].astype(jnp.int32) // CAP
        others = (others + (others >= busiest).astype(jnp.int32)).astype(jnp.int32)
        assigned = jnp.concatenate([jnp.full((CAP,), busiest, dtype=jnp.int32), others])
        return jax.random.permutation(third_key, assigned).astype(jnp.int32)
    return jax.vmap(one_row)(jax.random.split(jax.random.fold_in(key, 41), 4))


def with_ends(drawn, stream_key, least, high):
    index_at = [jax.random.randint(jax.random.fold_in(stream_key, axis), (), 0, length) for axis, length in enumerate(drawn.shape)]
    longest = drawn.shape.index(max(drawn.shape))
    next_to = index_at[:longest] + [(index_at[longest] + 1) % drawn.shape[longest]] + index_at[longest + 1:]
    return drawn.at[tuple(index_at)].set(least).at[tuple(next_to)].set(high)


def block_scale(own_key, shape, cuts, smallest, largest):
    loudness = 1.0
    for position, shards_of in cuts:
        draws = jax.random.uniform(jax.random.fold_in(jax.random.fold_in(own_key, 6), position), (shards_of,), jnp.float32, smallest / len(cuts), largest / len(cuts))
        loudness = loudness * jnp.repeat(jnp.exp(draws), shape[position] // shards_of).reshape((-1,) + (1,) * (len(shape) - 1 - position))
    return loudness


def centred(stream_key, extent, scale, bound, cuts=(), held_as=jnp.bfloat16):
    result = jax.random.normal(stream_key, extent, jnp.float32) * scale
    if len(cuts) > 0:
        result = block_scale(stream_key, extent, cuts, -0.22, 0.18) * result
    return jnp.clip(result, min=-bound, max=bound).astype(held_as)


def setup_inputs(seed: int = 0) -> dict:
    key_of = jax.random.split(jax.random.key(seed), 13)
    return {
        "coeffs": centred(key_of[0], (A0, NH, 4, R, NV), 1.0, 6.0, ((1, 32), (2, 4)), jnp.float32),
        "skeleton_first": draw_skeleton_first(jax.random.fold_in(key_of[12], 71), 0),
        "skeleton_second": draw_skeleton_second(jax.random.fold_in(key_of[12], 71), 0),
        "skeleton_third": draw_skeleton_third(jax.random.fold_in(key_of[12], 71), 0),
        "checks_first": draw_checks_first(jax.random.fold_in(key_of[12], 71), 0),
        "checks_second": draw_checks_second(jax.random.fold_in(key_of[12], 71), 0),
        "checks_third": draw_checks_third(jax.random.fold_in(key_of[12], 71), 0),
        "ranks_first": with_ends(jax.random.randint(key_of[7], (A0, NH, 4), R // 2, R + 1), jax.random.fold_in(key_of[7], 1), R // 2, R).astype(jnp.int32),
        "ranks_second": with_ends(jax.random.randint(key_of[8], (A0, NH, 4), R // 2, R + 1), jax.random.fold_in(key_of[8], 1), R // 2, R).astype(jnp.int32),
        "ranks_third": with_ends(jax.random.randint(key_of[9], (A0, 4, 2, NB), R // 2, R + 1), jax.random.fold_in(key_of[9], 1), R // 2, R).astype(jnp.int32),
        "interpolants": centred(key_of[10], (3, R, R), (R * R) ** -0.5, 0.09375, (), jnp.float32),
        "owners": draw_owners(jax.random.fold_in(key_of[12], 71), 0),
    }


two_pi = 2.0 * math.pi
highest = lax.Precision.HIGHEST


def kernel_block(targets, sources):
    target_rows = targets[..., :, None]
    source_cols = sources[..., None, :]
    upper_part = target_rows // 1024
    lower_part = target_rows % 1024
    phases = ((upper_part * source_cols) % 1024 * 1024 + lower_part * source_cols) % NPTS
    return jnp.cos(phases.astype(jnp.float32) * (two_pi / NPTS))


def merge_block(checks, points, stacked, matrix, rank_rows):
    kernels = kernel_block(checks, points)
    images = jnp.einsum('...cs,...sn->...cn', kernels, stacked, precision=highest)
    rank_width = matrix.shape[0]
    images = images.reshape(images.shape[:-2] + (images.shape[-2] // rank_width, rank_width, images.shape[-1]))
    merged = jnp.einsum('ij,...tjn->...tin', matrix, images, precision=highest)
    live_rows = jnp.arange(rank_width, dtype=jnp.int32) < rank_rows[..., None]
    return jnp.where(live_rows[..., None], merged, 0.0)


def apply_level(checks, points, stacked, matrix, rank_rows):
    def one_parent(pieces):
        check_row, point_rows, coeff_rows, rank_part = pieces
        spread = jnp.broadcast_to(check_row, (point_rows.shape[0],) + check_row.shape)
        return merge_block(spread, point_rows, coeff_rows, matrix, rank_part)
    return lax.map(one_parent, (checks, points, stacked, rank_rows))


def slot_table(owner_row, box_count, capacity):
    parent_count = owner_row.shape[0]
    onehot = (owner_row[:, None] == jnp.arange(box_count, dtype=jnp.int32)[None, :]).astype(jnp.int32)
    earlier = jnp.cumsum(onehot, axis=0, dtype=jnp.int32) - onehot
    slot_of = jnp.sum(earlier * onehot, axis=1, dtype=jnp.int32)
    matches = (onehot.T[:, None, :] == 1) & (slot_of[None, None, :] == jnp.arange(capacity, dtype=jnp.int32)[None, :, None])
    slot_parent = jnp.sum(jnp.where(matches, jnp.arange(parent_count, dtype=jnp.int32)[None, None, :], 0), axis=2).astype(jnp.int32)
    slot_used = jnp.any(matches, axis=2)
    return slot_parent, slot_used


def reference(coeffs, skeleton_first, skeleton_second, skeleton_third, checks_first, checks_second, checks_third, ranks_first, ranks_second, ranks_third, interpolants, owners):
    local_boxes = jnp.arange(NH, dtype=jnp.int32)[None, :, None, None]
    four_slots = jnp.arange(4, dtype=jnp.int32)[None, None, :, None]
    points_first = (4 * local_boxes + 2 * (four_slots % 2) + four_slots // 2) * (NPTS // (4 * NH)) + skeleton_first
    points_second = (2 * local_boxes + four_slots % 2) * (NPTS // (2 * NH)) + skeleton_second
    points_third = local_boxes * (NPTS // NH) + skeleton_third
    targets_first = jnp.arange(2 * A0, dtype=jnp.int32)[:, None] * (NPTS // (2 * A0)) + checks_first
    targets_second = jnp.arange(4 * A0, dtype=jnp.int32)[:, None] * (NPTS // (4 * A0)) + checks_second
    targets_third = jnp.arange(8 * A0, dtype=jnp.int32)[:, None] * (NPTS // (8 * A0)) + checks_third

    level_one = []
    for member in range(4):
        lowbit = member % 2
        highbit = member // 2
        points = jnp.concatenate([points_first[:, :, lowbit], points_first[:, :, 2 + lowbit]], axis=2)
        stacked = jnp.concatenate([coeffs[:, :, lowbit], coeffs[:, :, 2 + lowbit]], axis=2)
        checks = targets_first.reshape(A0, 2, R)[:, highbit]
        level_one.append(apply_level(checks, points, stacked, interpolants[0], ranks_first[:, :, member, None]))
    merged_one = jnp.concatenate(level_one, axis=2)

    level_two = []
    for member in range(4):
        first_of = 2 * (member // 2)
        points = jnp.concatenate([points_second[:, :, first_of], points_second[:, :, first_of + 1]], axis=2)
        stacked = jnp.concatenate([merged_one[:, :, first_of], merged_one[:, :, first_of + 1]], axis=2)
        checks = targets_second.reshape(A0, 4, R)[:, member]
        level_two.append(apply_level(checks, points, stacked, interpolants[1], ranks_second[:, :, member, None]))
    merged_two = jnp.concatenate(level_two, axis=2)

    outputs = []
    for member in range(4):
        points = points_third[:, :, member].reshape(A0, NB, 2 * R)
        stacked = merged_two[:, :, member].reshape(A0, NB, 2 * R, NV)
        checks = targets_third.reshape(A0, 4, 2 * R)[:, member]
        rank_rows = jnp.transpose(ranks_third[:, member], (0, 2, 1))
        merged = apply_level(checks, points, stacked, interpolants[2], rank_rows)
        slot_parent, slot_used = slot_table(owners[member], NB, CAP)
        picked = jnp.take(merged, slot_parent, axis=0)
        picked = jnp.where(slot_used[:, :, None, None, None, None], picked, 0.0)
        outputs.append(jnp.transpose(picked, (0, 3, 1, 2, 4, 5)))
    return jnp.stack(outputs, axis=0)
```

```python
import functools

import jax
import jax.numpy as jnp
import numpy as np
from jax import lax
from jax.experimental import pallas as pl
from jax.experimental.pallas import tpu as pltpu
from jax.sharding import PartitionSpec as P

NPTS = 1048576
R = 64
A0 = 64
HALF_A = 32
LANES = 128
CAP = 4
MESH = pl.DeviceIdType.MESH
f32 = jnp.float32
bf16 = jnp.bfloat16

SIN_COEFFS = (
    6.2831851600873945,
    -41.34165503088491,
    81.60100403766654,
    -76.54978142785076,
    39.53669915281796,
)

CHIP_STEPS = (
    (1, 0), (0, 1), (3, 0), (0, 3), (1, 1), (3, 3), (1, 3), (3, 1),
    (2, 1), (1, 2), (2, 3), (3, 2), (2, 0), (0, 2), (2, 2),
)


def split(value):
    high = value.astype(bf16)
    low = (value - high.astype(f32)).astype(bf16)
    return high, low


def dot(left, right):
    return jnp.dot(left, right, preferred_element_type=f32)


def dot3(left, right):
    return dot(left[0], right[0]) + dot(left[1], right[0]) + dot(left[0], right[1])


def cosines(scaled_rows, columns):
    phases = (scaled_rows * columns).astype(f32)
    turn = 0.25 - jnp.abs(phases) * (2.0**-32)
    square = turn * turn
    total = SIN_COEFFS[4]
    for coeff in SIN_COEFFS[3::-1]:
        total = total * square + coeff
    return total * turn


def operators_kernel(cols_ref, rows_ref, mats_ref, high_ref, low_ref, q12, q33, mask4, mask2):
    @pl.when(pl.program_id(0) == 0)
    def _():
        zero = jnp.zeros((R, R), f32)

        def pair(first, second):
            return jnp.concatenate(
                [jnp.concatenate([first, zero], axis=1), jnp.concatenate([zero, second], axis=1)],
                axis=0,
            )

        for ref, first, second in ((q12, 0, 1), (q33, 2, 2)):
            high, low = split(pair(mats_ref[first], mats_ref[second]))
            ref[0] = high
            ref[1] = low
        row4 = lax.broadcasted_iota(jnp.int32, (256, 256), 0) // R
        col4 = lax.broadcasted_iota(jnp.int32, (256, 256), 1) // R
        mask4[...] = jnp.where(row4 == col4, 1.0, 0.0).astype(bf16)
        row2 = lax.broadcasted_iota(jnp.int32, (128, 256), 0) // R
        col2 = lax.broadcasted_iota(jnp.int32, (128, 256), 1) // LANES
        mask2[...] = jnp.where(row2 == col2, 1.0, 0.0).astype(bf16)

    rank_row = lax.broadcasted_iota(jnp.int32, (R, 256), 0)
    half_row = lax.broadcasted_iota(jnp.int32, (LANES, LANES), 0)
    for target in range(2):
        x12 = jnp.broadcast_to(rows_ref[0, 2 * target : 2 * target + 1, :], (LANES, LANES)).T
        x3 = jnp.broadcast_to(rows_ref[0, 2 * target + 1 : 2 * target + 2, :], (LANES, LANES)).T
        x12 = jnp.concatenate([x12, x12], axis=1)
        k1 = cosines(x12[:R], cols_ref[0, 0:1, :])
        k2 = cosines(x12[R:], cols_ref[0, 1 + target : 2 + target, :])
        k3 = cosines(x3, cols_ref[0, 3:4, target * LANES : (target + 1) * LANES])
        mixed = dot3((q12[0], q12[1]), split(jnp.concatenate([k1, k2], axis=0)))
        live1 = rank_row < cols_ref[0, 4 + target : 5 + target, :]
        live2 = rank_row < cols_ref[0, 6 + target : 7 + target, :]
        first = split(jnp.where(live1, mixed[:R], 0.0))
        second = split(jnp.where(live2, mixed[R:], 0.0))
        blocks = tuple(jnp.concatenate([part] * 4, axis=0) * mask4[...] for part in first)
        merged = split(dot3(second, blocks))
        stacked = tuple(jnp.concatenate([part] * 2, axis=0) * mask2[...] for part in merged)
        third = dot3((q33[0], q33[1]), split(k3))
        rank3 = jnp.where(
            half_row < R,
            rows_ref[0, 4 + 2 * target : 5 + 2 * target, :],
            rows_ref[0, 5 + 2 * target : 6 + 2 * target, :] + R,
        )
        third = split(jnp.where(half_row < rank3, third, 0.0))
        high, low = split(dot3(third, stacked))
        high_ref[0, target] = high
        low_ref[0, target] = low


def build_operators(cols, rows, mats):
    shape = jax.ShapeDtypeStruct((A0, 2, LANES, 256), bf16)
    block = pl.BlockSpec((1, 2, LANES, 256), lambda a: (a, 0, 0, 0))
    return pl.pallas_call(
        operators_kernel,
        grid=(A0,),
        out_shape=(shape, shape),
        in_specs=[
            pl.BlockSpec((1, 8, 256), lambda a: (a, 0, 0)),
            pl.BlockSpec((1, 8, LANES), lambda a: (a, 0, 0)),
            pl.BlockSpec((3, R, R), lambda a: (0, 0, 0)),
        ],
        out_specs=(block, block),
        scratch_shapes=[
            pltpu.VMEM((2, LANES, LANES), bf16),
            pltpu.VMEM((2, LANES, LANES), bf16),
            pltpu.VMEM((256, 256), bf16),
            pltpu.VMEM((LANES, 256), bf16),
        ],
        cost_estimate=pl.CostEstimate(
            flops=5_000_000_000, bytes_accessed=17_000_000, transcendentals=0
        ),
    )(cols, rows, mats)


def peer_of(box, step):
    row = lax.rem(box // 8 + step // 8, 4)
    col = lax.rem((box // 2) % 4 + (step // 2) % 4, 4)
    core = lax.rem(box % 2 + step % 2, 2)
    return row * 8 + col * 2 + core


def exchange_kernel(
    coeffs, near_even, near_odd, high, low, parents, used, out,
    w_high, w_low, own, near_a, near_b, partial, stage,
    send_a0, send_a1, send_b0, send_b1, recv_a0, recv_a1, recv_b0, recv_b1,
    load_sem, own_sem, near_send, near_recv, part_send, part_recv, msg_send, msg_recv, self_sem,
):
    tbit = lax.axis_index("tbit")
    box = lax.axis_index("box")
    by_low = tbit + 1 - 2 * (tbit % 2)
    by_both = 3 - tbit
    sends = ((send_a0, send_a1), (send_b0, send_b1))
    recvs = ((recv_a0, recv_a1), (recv_b0, recv_b1))

    def eight(group):
        return pl.ds(pl.multiple_of(group * 8, 8), 8)

    def load_operator(group):
        rows = eight(group)
        return (
            pltpu.make_async_copy(high.at[rows], w_high.at[rows], load_sem.at[0, group]),
            pltpu.make_async_copy(low.at[rows], w_low.at[rows], load_sem.at[1, group]),
        )

    def load_own(half, group):
        rows = eight(group)
        lanes = pl.ds(half * LANES, LANES)
        return pltpu.make_async_copy(
            coeffs.at[rows, :, :, lanes], own.at[rows], own_sem.at[half, group]
        )

    def load_near(group):
        side = near_even if group < 4 else near_odd
        return pltpu.make_async_copy(
            side.at[pl.ds((group % 4) * 8, 8)],
            near_a.at[pl.ds(group * 8, 8)],
            load_sem.at[2, group],
        )

    for group in range(8):
        for copy in load_operator(group):
            copy.start()
        load_own(0, group).start()
        load_near(group).start()

    barrier = pltpu.get_barrier_semaphore()

    def greet(step, _):
        pl.semaphore_signal(
            barrier, inc=1, device_id=(tbit, peer_of(box, step)), device_id_type=MESH
        )
        return 0

    lax.fori_loop(1, 32, greet, 0)
    for side in (by_low, by_both):
        pl.semaphore_signal(barrier, inc=1, device_id=(side, box), device_id_type=MESH)
    pl.semaphore_wait(barrier, 33)

    def send_near(group):
        upper = group // 4
        rows = eight(group)
        return pltpu.make_async_remote_copy(
            src_ref=coeffs.at[rows, :, :, pl.ds(LANES, LANES)],
            dst_ref=near_b.at[rows],
            send_sem=near_send.at[group],
            recv_sem=near_recv.at[group],
            device_id=((1 - upper) * by_low + upper * by_both, box),
            device_id_type=MESH,
        )

    def send_partial(half, t, group):
        upper = group // 4
        rows = eight(group)
        return pltpu.make_async_remote_copy(
            src_ref=sends[half][t].at[rows],
            dst_ref=recvs[half][t].at[rows],
            send_sem=part_send.at[half, t, group],
            recv_sem=part_recv.at[half, t, group],
            device_id=((1 - upper) * by_both + upper * by_low, box),
            device_id_type=MESH,
        )

    def multiply(half, near, group):
        def one(member, _):
            a = group * 8 + member
            points = split(
                jnp.concatenate([own[a, 0], near[a, 0], own[a, 1], near[a, 1]], axis=0)
            )
            left = (w_high[a].reshape(256, 256), w_low[a].reshape(256, 256))
            result = dot3(left, points)
            partial[a] = result[:LANES].reshape(2, R, LANES)
            sends[half][0][a] = result[LANES : LANES + R]
            sends[half][1][a] = result[LANES + R :]
            return 0

        lax.fori_loop(0, 8, one, 0)

    def message(half, t, step):
        return pltpu.make_async_remote_copy(
            src_ref=stage.at[t, step],
            dst_ref=out.at[t, :, box, :, pl.ds(half * LANES, LANES)],
            send_sem=msg_send.at[half, t, step],
            recv_sem=msg_recv.at[half, t, step],
            device_id=(tbit, peer_of(box, step)),
            device_id_type=MESH,
        )

    def keep(half, t):
        return pltpu.make_async_copy(
            stage.at[t, 0],
            out.at[t, :, box, :, pl.ds(half * LANES, LANES)],
            self_sem.at[half, t],
        )

    def fill(half, t, step):
        owner = peer_of(box, step)
        for slot in range(CAP):
            parent = parents[owner * CAP + slot]
            live = used[owner * CAP + slot]
            value = partial[parent, t] + recvs[half][t][parent]
            stage[t, step, slot] = jnp.where(jnp.full((R, LANES), live) > 0, value, 0.0)

    def release(half, t):
        for group in range(8):
            send_partial(half, t, group).wait_recv()
        if half == 1:
            keep(0, t).wait()

        def go(step):
            if half == 1:
                message(0, t, step).wait_send()
            fill(half, t, step)
            message(half, t, step).start()

        go(1)
        for core in range(2):
            for row, col in CHIP_STEPS:
                go(row * 8 + col * 2 + core)
        fill(half, t, 0)
        keep(half, t).start()

    for group in range(8):
        for copy in load_operator(group):
            copy.wait()
        load_own(0, group).wait()
        load_near(group).wait()
        multiply(0, near_a, group)
        load_own(1, group).start()
        send_partial(0, 0, group).start()
    for group in range(8):
        send_partial(0, 1, group).start()
    for group in range(8):
        send_near(group).start()
    release(0, 0)
    release(0, 1)

    for group in range(8):
        load_own(1, group).wait()
        send_near(group).wait_recv()
        multiply(1, near_b, group)
        send_partial(1, 0, group).start()
    for group in range(8):
        send_partial(1, 1, group).start()
    release(1, 0)
    release(1, 1)

    for t in range(2):
        keep(1, t).wait()

        def finish(step, _):
            message(1, t, step).wait_send()
            message(0, t, step).wait_recv()
            message(1, t, step).wait_recv()
            return 0

        lax.fori_loop(1, 32, finish, 0)
    for group in range(8):
        send_near(group).wait_send()
        for half in range(2):
            for t in range(2):
                send_partial(half, t, group).wait_send()


def exchange(coeffs, near_even, near_odd, high, low, parents, used):
    hbm = pl.BlockSpec(memory_space=pl.ANY)
    smem = pl.BlockSpec(memory_space=pltpu.SMEM)
    part = pltpu.VMEM((A0, R, LANES), f32)
    halves = pltpu.VMEM((A0, 2, R, LANES), f32)
    dma = pltpu.SemaphoreType.DMA
    return pl.pallas_call(
        exchange_kernel,
        out_shape=jax.ShapeDtypeStruct((2, CAP, 32, R, 256), f32),
        in_specs=[hbm] * 5 + [smem] * 2,
        out_specs=hbm,
        scratch_shapes=[
            pltpu.VMEM((A0, 2, LANES, 256), bf16),
            pltpu.VMEM((A0, 2, LANES, 256), bf16),
            halves, halves, halves, halves,
            pltpu.VMEM((2, 32, CAP, R, LANES), f32),
        ]
        + [part] * 8
        + [
            dma((3, 8)), dma((2, 8)), dma((8,)), dma((8,)),
            dma((2, 2, 8)), dma((2, 2, 8)), dma((2, 2, 32)), dma((2, 2, 32)), dma((2, 2)),
        ],
        compiler_params=pltpu.CompilerParams(
            collective_id=0, has_side_effects=True, vmem_limit_bytes=62 << 20
        ),
    )(coeffs, near_even, near_odd, high, low, parents, used)


def slot_table(owner_row, box_count, capacity):
    parent_count = owner_row.shape[0]
    onehot = (owner_row[:, None] == jnp.arange(box_count, dtype=jnp.int32)[None, :]).astype(
        jnp.int32
    )
    earlier = jnp.cumsum(onehot, axis=0, dtype=jnp.int32) - onehot
    slot_of = jnp.sum(earlier * onehot, axis=1, dtype=jnp.int32)
    matches = (onehot.T[:, None, :] == 1) & (
        slot_of[None, None, :] == jnp.arange(capacity, dtype=jnp.int32)[None, :, None]
    )
    slot_parent = jnp.sum(
        jnp.where(matches, jnp.arange(parent_count, dtype=jnp.int32)[None, None, :], 0), axis=2
    )
    slot_used = jnp.any(matches, axis=2)
    return (slot_parent, slot_used)


def by_parent(values, axis, even, odd):
    return jnp.concatenate(
        [
            lax.dynamic_index_in_dim(values[:HALF_A], even, axis, keepdims=False),
            lax.dynamic_index_in_dim(values[HALF_A:], odd, axis, keepdims=False),
        ],
        axis=0,
    )


def tables(
    tbit, box, skeleton_first, skeleton_second, skeleton_third,
    checks_first, checks_second, checks_third, ranks_first, ranks_second, ranks_third,
):
    local_boxes = 2 * box + jnp.arange(2, dtype=jnp.int32)[None, :, None, None]
    four = jnp.arange(4, dtype=jnp.int32)[None, None, :, None]
    points_first = (4 * local_boxes + 2 * (four % 2) + four // 2) * (NPTS // 256) + skeleton_first
    points_second = (2 * local_boxes + four % 2) * (NPTS // 128) + skeleton_second
    points_third = local_boxes * (NPTS // 64) + skeleton_third
    parent = jnp.arange(A0, dtype=jnp.int32)
    low, high, both = tbit ^ 1, tbit ^ 2, tbit ^ 3
    group = tbit // 2
    ranks = jnp.moveaxis(
        lax.all_gather(jnp.stack([ranks_first[:, :, 0], ranks_second[:, :, 0]]), "tbit"), 0, -1
    )

    def wide(values):
        return jnp.broadcast_to(values, (A0, 2, 2, R)).reshape(A0, 256)

    def both_sources(values, axis, first, second):
        return jnp.stack(
            [by_parent(values, axis, *first), by_parent(values, axis, *second)], axis=2
        )

    own, other = (tbit, tbit), (both, low)
    first_slots = ((tbit, tbit), (low, low))
    other_slots = ((high, tbit), (both, low))
    row0 = both_sources(points_first, 2, (tbit, tbit), (low, both)).reshape(A0, 256)
    row1 = both_sources(points_second, 2, *first_slots).reshape(A0, 256)
    row2 = both_sources(points_second, 2, *other_slots).reshape(A0, 256)
    row3 = jnp.concatenate(
        [by_parent(points_third, 2, *side).reshape(A0, 128) for side in (own, other)], axis=1
    )
    row4 = wide(both_sources(ranks[0], 2, *first_slots)[..., None])
    row5 = wide(both_sources(ranks[0], 2, *other_slots)[..., None])
    row6 = wide(by_parent(ranks[1], 2, *own)[:, :, None, None])
    row7 = wide(by_parent(ranks[1], 2, *other)[:, :, None, None])
    columns = jnp.stack([row0, row1, row2, row3, row4, row5, row6, row7], axis=1)

    targets_first = (
        jnp.arange(2 * A0, dtype=jnp.int32)[:, None] * (NPTS // (2 * A0)) + checks_first
    ).reshape(A0, 2, R)
    targets_second = (
        jnp.arange(4 * A0, dtype=jnp.int32)[:, None] * (NPTS // (4 * A0)) + checks_second
    ).reshape(A0, 4, R)
    targets_third = (
        jnp.arange(8 * A0, dtype=jnp.int32)[:, None] * (NPTS // (8 * A0)) + checks_third
    ).reshape(A0, 4, 2 * R)
    ranks_mine = lax.dynamic_index_in_dim(ranks_third, box, 3, keepdims=False)
    rows, limits = [], []
    for side, groups in ((own, (group, group)), (other, (1 - group, group))):
        rows.append(
            jnp.concatenate(
                [by_parent(targets_first, 1, *groups), by_parent(targets_second, 1, *side)],
                axis=1,
            )
            * 4096
        )
        rows.append(by_parent(targets_third, 1, *side) * 4096)
        limit = by_parent(ranks_mine, 1, *side)
        limits += [jnp.broadcast_to(limit[:, t : t + 1], (A0, LANES)) for t in range(2)]
    return columns, jnp.stack(rows + limits, axis=1)


def per_device(
    coeffs,
    skeleton_first,
    skeleton_second,
    skeleton_third,
    checks_first,
    checks_second,
    checks_third,
    ranks_first,
    ranks_second,
    ranks_third,
    interpolants,
    owners,
):
    tbit = lax.axis_index("tbit")
    box = lax.axis_index("box")
    coeffs = coeffs[:, :, 0]
    near_even = lax.ppermute(
        coeffs[:HALF_A, :, :, :LANES], "tbit", [(k, k ^ 1) for k in range(4)]
    )
    near_odd = lax.ppermute(
        coeffs[HALF_A:, :, :, :LANES], "tbit", [(k, k ^ 3) for k in range(4)]
    )
    columns, rows = tables(
        tbit, box, skeleton_first, skeleton_second, skeleton_third,
        checks_first, checks_second, checks_third, ranks_first, ranks_second, ranks_third,
    )
    high, low = build_operators(columns, rows, interpolants)
    slot_parent, slot_used = slot_table(
        lax.dynamic_index_in_dim(owners, tbit, 0, keepdims=False), 32, CAP
    )
    switched = exchange(
        coeffs, near_even, near_odd, high, low,
        slot_parent.reshape(-1), slot_used.reshape(-1).astype(jnp.int32),
    )
    return switched[None, None]


def solution(mesh):
    return jax.shard_map(
        per_device,
        mesh=mesh,
        in_specs=(
            P(None, "box", "tbit", None, None),
            P(None, "box", None, None),
            P(None, "box", None, None),
            P(None, "box", None, None),
            P(),
            P(),
            P(),
            P(None, "box", "tbit"),
            P(None, "box", "tbit"),
            P(),
            P(),
            P(),
        ),
        out_specs=P("tbit", "box", None, None, None, None, None),
        check_vma=False,
    )
```

```python
import functools

import jax
import jax.numpy as jnp
import numpy as np
from jax import lax
from jax.experimental import pallas as pl
from jax.experimental.pallas import tpu as pltpu
from jax.sharding import PartitionSpec as P

NPTS = 1048576
R = 64
A0 = 64
HALF_A = 32
LANES = 128
GROUP = 8
BATCH = 8
UNROLL = 4
CAP = 4
MESH = pl.DeviceIdType.MESH
f32 = jnp.float32
bf16 = jnp.bfloat16

SIN_COEFFS = (
    6.2831851600873945,
    -41.34165503088491,
    81.60100403766654,
    -76.54978142785076,
    39.53669915281796,
)

CHIP_STEPS = (
    (1, 0), (0, 1), (3, 0), (0, 3), (1, 1), (3, 3), (1, 3), (3, 1),
    (2, 1), (1, 2), (2, 3), (3, 2), (2, 0), (0, 2), (2, 2),
)

PIECES = ((0, 0, 32), (0, 32, 32), (1, 0, 64))


def split(value):
    high = value.astype(bf16)
    low = (value - high.astype(f32)).astype(bf16)
    return high, low


def dot(left, right):
    return jnp.dot(left, right, preferred_element_type=f32)


def dot3(left, right):
    return dot(left[0], right[0]) + dot(left[1], right[0]) + dot(left[0], right[1])


def cosines(scaled_rows, columns):
    phases = (scaled_rows * columns).astype(f32)
    turn = 0.25 - jnp.abs(phases) * (2.0**-32)
    square = turn * turn
    total = SIN_COEFFS[4]
    for coeff in SIN_COEFFS[3::-1]:
        total = total * square + coeff
    return total * turn


def operators_kernel(cols_ref, rows_ref, mats_ref, high_ref, low_ref, mats, mask4, mask2):
    @pl.when(pl.program_id(0) == 0)
    def _():
        for level in range(3):
            high, low = split(mats_ref[level])
            mats[level] = jnp.concatenate([high, low, high, low], axis=1)
        row4 = lax.broadcasted_iota(jnp.int32, (256, 256), 0) // R
        col4 = lax.broadcasted_iota(jnp.int32, (256, 256), 1) // R
        mask4[...] = jnp.where(row4 == col4, 1.0, 0.0).astype(bf16)
        row2 = lax.broadcasted_iota(jnp.int32, (128, 256), 0) // R
        col2 = lax.broadcasted_iota(jnp.int32, (128, 256), 1) // LANES
        mask2[...] = jnp.where(row2 == col2, 1.0, 0.0).astype(bf16)

    rank_row = lax.broadcasted_iota(jnp.int32, (R, 256), 0)
    rank_half = lax.broadcasted_iota(jnp.int32, (R, LANES), 0)

    def doubled(kernel):
        high, low = split(kernel)
        return jnp.concatenate([high, high, low, low], axis=0)

    def masked(value, member, row):
        return split(jnp.where(rank_row < cols_ref[member, row : row + 1, :], value, 0.0))

    def cut(value, member, row):
        halves = [
            jnp.where(
                rank_half < rows_ref[member, row + t : row + t + 1, :],
                value[:, t * LANES : (t + 1) * LANES],
                0.0,
            )
            for t in range(2)
        ]
        return split(jnp.concatenate(halves, axis=0))

    def batch(units):
        points = []
        for member, target in units:
            x12 = rows_ref[member, 2 * target : 2 * target + 1, :]
            x12 = jnp.broadcast_to(x12, (LANES, LANES)).T
            x3 = rows_ref[member, 2 * target + 1 : 2 * target + 2, :]
            points.append(
                (jnp.concatenate([x12, x12], axis=1), jnp.broadcast_to(x3, (LANES, LANES)).T)
            )
        k1 = [
            doubled(cosines(p[0][:R], cols_ref[m, 0:1, :])) for p, (m, t) in zip(points, units)
        ]
        first = [dot(mats[0], k) for k in k1]
        k2 = [
            doubled(cosines(p[0][R:], cols_ref[m, 1 + t : 2 + t, :]))
            for p, (m, t) in zip(points, units)
        ]
        second = [dot(mats[1], k) for k in k2]
        k3 = [
            cosines(p[1], cols_ref[m, 3:4, t * LANES : (t + 1) * LANES])
            for p, (m, t) in zip(points, units)
        ]
        k3 = [doubled(jnp.concatenate([k[:R], k[R:]], axis=1)) for k in k3]
        third = [dot(mats[2], k) for k in k3]
        first = [masked(v, m, 4 + t) for v, (m, t) in zip(first, units)]
        blocks = [
            tuple(jnp.concatenate([part] * 4, axis=0) * mask4[...] for part in v) for v in first
        ]
        second = [masked(v, m, 6 + t) for v, (m, t) in zip(second, units)]
        merged = [dot(jnp.concatenate(v, axis=0), b[0]) for v, b in zip(second, blocks)]
        extra = [dot(v[0], b[1]) for v, b in zip(second, blocks)]
        third = [cut(v, m, 4 + 2 * t) for v, (m, t) in zip(third, units)]
        merged = [split(v[:R] + v[R:] + e) for v, e in zip(merged, extra)]
        stacked = [
            tuple(jnp.concatenate([part] * 2, axis=0) * mask2[...] for part in v) for v in merged
        ]
        main = [
            dot(jnp.concatenate(v, axis=1), jnp.concatenate([b[0]] * 2, axis=0))
            for v, b in zip(third, stacked)
        ]
        rest = [dot(v[0], b[1]) for v, b in zip(third, stacked)]
        for v, e, (member, target) in zip(main, rest, units):
            high, low = split(v + e)
            high_ref[member, target] = high
            low_ref[member, target] = low

    units = [(m, t) for m in range(GROUP) for t in range(2)]
    for begin in range(0, len(units), BATCH):
        batch(units[begin : begin + BATCH])


def build_operators(cols, rows, mats):
    shape = jax.ShapeDtypeStruct((A0, 2, LANES, 256), bf16)
    block = pl.BlockSpec((GROUP, 2, LANES, 256), lambda a: (a, 0, 0, 0))
    return pl.pallas_call(
        operators_kernel,
        grid=(A0 // GROUP,),
        out_shape=(shape, shape),
        in_specs=[
            pl.BlockSpec((GROUP, 8, 256), lambda a: (a, 0, 0)),
            pl.BlockSpec((GROUP, 8, LANES), lambda a: (a, 0, 0)),
            pl.BlockSpec((3, R, R), lambda a: (0, 0, 0)),
        ],
        out_specs=(block, block),
        scratch_shapes=[
            pltpu.VMEM((3, R, 256), bf16),
            pltpu.VMEM((256, 256), bf16),
            pltpu.VMEM((LANES, 256), bf16),
        ],
        cost_estimate=pl.CostEstimate(
            flops=20_000_000_000, bytes_accessed=17_000_000, transcendentals=0
        ),
    )(cols, rows, mats)


def peer_of(box, step):
    row = lax.rem(box // 8 + step // 8, 4)
    col = lax.rem((box // 2) % 4 + (step // 2) % 4, 4)
    core = lax.rem(box % 2 + step % 2, 2)
    return row * 8 + col * 2 + core


def exchange_kernel(
    coeffs, near_even, near_odd, high, low, parents, used, out,
    w_high, w_low, own, near_a, near_b, partial, *rest,
):
    count = len(PIECES)
    stages, sends, recvs = rest[:count], rest[count : 3 * count], rest[3 * count : 5 * count]
    (
        load_sem, own_sem, near_send, near_recv, part_send, part_recv,
        msg_send, msg_recv, self_sem,
    ) = rest[5 * count :]
    tbit = lax.axis_index("tbit")
    box = lax.axis_index("box")
    by_low = tbit + 1 - 2 * (tbit % 2)
    by_both = 3 - tbit

    def eight(group):
        return pl.ds(group * 8, 8)

    def load_operator(group):
        rows = eight(group)
        return (
            pltpu.make_async_copy(high.at[rows], w_high.at[rows], load_sem.at[0, group]),
            pltpu.make_async_copy(low.at[rows], w_low.at[rows], load_sem.at[1, group]),
        )

    def load_own(half, group):
        rows = eight(group)
        lanes = pl.ds(half * LANES, LANES)
        return pltpu.make_async_copy(
            coeffs.at[rows, :, :, lanes], own.at[rows], own_sem.at[half, group]
        )

    def load_near(group):
        side = near_even if group < 4 else near_odd
        return pltpu.make_async_copy(
            side.at[eight(group % 4)], near_a.at[eight(group)], load_sem.at[2, group]
        )

    for group in range(8):
        for copy in load_operator(group):
            copy.start()
        load_own(0, group).start()
        load_near(group).start()

    barrier = pltpu.get_barrier_semaphore()

    def greet(step, _):
        pl.semaphore_signal(
            barrier, inc=1, device_id=(tbit, peer_of(box, step)), device_id_type=MESH
        )
        return 0

    lax.fori_loop(1, 32, greet, 0)
    for side in (by_low, by_both):
        pl.semaphore_signal(barrier, inc=1, device_id=(side, box), device_id_type=MESH)
    pl.semaphore_wait(barrier, 33)

    def send_near(group):
        rows = eight(group)
        return pltpu.make_async_remote_copy(
            src_ref=coeffs.at[rows, :, :, pl.ds(LANES, LANES)],
            dst_ref=near_b.at[rows],
            send_sem=near_send.at[group],
            recv_sem=near_recv.at[group],
            device_id=(by_low if group < 4 else by_both, box),
            device_id_type=MESH,
        )

    def send_partial(half, piece, group):
        rows = eight(group)
        index = half * count + piece
        return pltpu.make_async_remote_copy(
            src_ref=sends[index].at[rows],
            dst_ref=recvs[index].at[rows],
            send_sem=part_send.at[index, group],
            recv_sem=part_recv.at[index, group],
            device_id=(by_both if group < 4 else by_low, box),
            device_id_type=MESH,
        )

    def multiply(half, near, group):
        def some(batch, _):
            members = [group * 8 + batch * UNROLL + k for k in range(UNROLL)]
            points = [
                split(jnp.concatenate([own[a, 0], near[a, 0], own[a, 1], near[a, 1]], axis=0))
                for a in members
            ]
            highs = [w_high[a].reshape(256, 256) for a in members]
            main = [
                dot(jnp.concatenate([h, w_low[a].reshape(256, 256)], axis=0), p[0])
                for h, a, p in zip(highs, members, points)
            ]
            extra = [dot(h, p[1]) for h, p in zip(highs, points)]
            for a, m, e in zip(members, main, extra):
                result = m[:256] + m[256:] + e
                partial[a] = result[:LANES].reshape(2, R, LANES)
                for piece, (t, begin, size) in enumerate(PIECES):
                    first = LANES + t * R + begin
                    sends[half * count + piece][a] = result[first : first + size]
            return 0

        lax.fori_loop(0, 8 // UNROLL, some, 0)

    def target(half, piece):
        t, begin, size = PIECES[piece]
        return out.at[t, :, box, pl.ds(begin, size), pl.ds(half * LANES, LANES)]

    def message(half, piece, step):
        index = half * count + piece
        return pltpu.make_async_remote_copy(
            src_ref=stages[piece].at[step],
            dst_ref=target(half, piece),
            send_sem=msg_send.at[index, step],
            recv_sem=msg_recv.at[index, step],
            device_id=(tbit, peer_of(box, step)),
            device_id_type=MESH,
        )

    def keep(half, piece):
        return pltpu.make_async_copy(
            stages[piece].at[0], target(half, piece), self_sem.at[half, piece]
        )

    def fill(half, piece, step):
        t, begin, size = PIECES[piece]
        owner = peer_of(box, step)
        for slot in range(CAP):
            parent = parents[owner * CAP + slot]
            live = used[owner * CAP + slot]
            value = partial[parent, t, begin : begin + size]
            value = value + recvs[half * count + piece][parent]
            stages[piece][step, slot] = jnp.where(jnp.full((size, LANES), live) > 0, value, 0.0)

    def release(half, piece):
        for group in range(8):
            send_partial(half, piece, group).wait_recv()
        if half == 1:
            keep(0, piece).wait()

        def go(step):
            if half == 1:
                message(0, piece, step).wait_send()
            fill(half, piece, step)
            message(half, piece, step).start()

        go(1)
        for core in range(2):
            for row, col in CHIP_STEPS:
                go(row * 8 + col * 2 + core)
        fill(half, piece, 0)
        keep(half, piece).start()

    for group in range(8):
        for copy in load_operator(group):
            copy.wait()
        load_own(0, group).wait()
        load_near(group).wait()
        multiply(0, near_a, group)
        load_own(1, group).start()
        send_partial(0, 0, group).start()
    for piece in range(1, count):
        for group in range(8):
            send_partial(0, piece, group).start()
    for group in range(8):
        send_near(group).start()
    for piece in range(count):
        release(0, piece)

    for group in range(8):
        load_own(1, group).wait()
        send_near(group).wait_recv()
        multiply(1, near_b, group)
        send_partial(1, 0, group).start()
    for piece in range(1, count):
        for group in range(8):
            send_partial(1, piece, group).start()
    for piece in range(count):
        release(1, piece)

    for piece in range(count):
        keep(1, piece).wait()

        def finish(step, _):
            message(1, piece, step).wait_send()
            message(0, piece, step).wait_recv()
            message(1, piece, step).wait_recv()
            return 0

        lax.fori_loop(1, 32, finish, 0)
    for group in range(8):
        send_near(group).wait_send()
        for half in range(2):
            for piece in range(count):
                send_partial(half, piece, group).wait_send()


def exchange(coeffs, near_even, near_odd, high, low, parents, used):
    hbm = pl.BlockSpec(memory_space=pl.ANY)
    smem = pl.BlockSpec(memory_space=pltpu.SMEM)
    count = len(PIECES)
    parts = [pltpu.VMEM((A0, size, LANES), f32) for _, _, size in PIECES]
    halves = pltpu.VMEM((A0, 2, R, LANES), f32)
    dma = pltpu.SemaphoreType.DMA
    return pl.pallas_call(
        exchange_kernel,
        out_shape=jax.ShapeDtypeStruct((2, CAP, 32, R, 256), f32),
        in_specs=[hbm] * 5 + [smem] * 2,
        out_specs=hbm,
        scratch_shapes=[
            pltpu.VMEM((A0, 2, LANES, 256), bf16),
            pltpu.VMEM((A0, 2, LANES, 256), bf16),
            halves, halves, halves, halves,
        ]
        + [pltpu.VMEM((32, CAP, size, LANES), f32) for _, _, size in PIECES]
        + parts * 4
        + [
            dma((3, 8)), dma((2, 8)), dma((8,)), dma((8,)),
            dma((2 * count, 8)), dma((2 * count, 8)),
            dma((2 * count, 32)), dma((2 * count, 32)), dma((2, count)),
        ],
        compiler_params=pltpu.CompilerParams(
            collective_id=0, has_side_effects=True, vmem_limit_bytes=62 << 20
        ),
    )(coeffs, near_even, near_odd, high, low, parents, used)


def slot_table(owner_row, box_count, capacity):
    parent_count = owner_row.shape[0]
    onehot = (owner_row[:, None] == jnp.arange(box_count, dtype=jnp.int32)[None, :]).astype(
        jnp.int32
    )
    earlier = jnp.cumsum(onehot, axis=0, dtype=jnp.int32) - onehot
    slot_of = jnp.sum(earlier * onehot, axis=1, dtype=jnp.int32)
    matches = (onehot.T[:, None, :] == 1) & (
        slot_of[None, None, :] == jnp.arange(capacity, dtype=jnp.int32)[None, :, None]
    )
    slot_parent = jnp.sum(
        jnp.where(matches, jnp.arange(parent_count, dtype=jnp.int32)[None, None, :], 0), axis=2
    )
    slot_used = jnp.any(matches, axis=2)
    return (slot_parent, slot_used)


def by_parent(values, axis, even, odd):
    return jnp.concatenate(
        [
            lax.dynamic_index_in_dim(values[:HALF_A], even, axis, keepdims=False),
            lax.dynamic_index_in_dim(values[HALF_A:], odd, axis, keepdims=False),
        ],
        axis=0,
    )


def tables(
    tbit, box, skeleton_first, skeleton_second, skeleton_third,
    checks_first, checks_second, checks_third, ranks, ranks_third,
):
    local_boxes = 2 * box + jnp.arange(2, dtype=jnp.int32)[None, :, None, None]
    four = jnp.arange(4, dtype=jnp.int32)[None, None, :, None]
    points_first = (4 * local_boxes + 2 * (four % 2) + four // 2) * (NPTS // 256) + skeleton_first
    points_second = (2 * local_boxes + four % 2) * (NPTS // 128) + skeleton_second
    points_third = local_boxes * (NPTS // 64) + skeleton_third
    parent = jnp.arange(A0, dtype=jnp.int32)
    low, high, both = tbit ^ 1, tbit ^ 2, tbit ^ 3
    group = tbit // 2

    def wide(values):
        return jnp.broadcast_to(values, (A0, 2, 2, R)).reshape(A0, 256)

    def both_sources(values, axis, first, second):
        return jnp.stack(
            [by_parent(values, axis, *first), by_parent(values, axis, *second)], axis=2
        )

    own, other = (tbit, tbit), (both, low)
    first_slots = ((tbit, tbit), (low, low))
    other_slots = ((high, tbit), (both, low))
    row0 = both_sources(points_first, 2, (tbit, tbit), (low, both)).reshape(A0, 256)
    row1 = both_sources(points_second, 2, *first_slots).reshape(A0, 256)
    row2 = both_sources(points_second, 2, *other_slots).reshape(A0, 256)
    row3 = jnp.concatenate(
        [by_parent(points_third, 2, *side).reshape(A0, 128) for side in (own, other)], axis=1
    )
    mine, by_low, by_high, by_both = ranks

    def halves(even, odd):
        return jnp.concatenate([even[:HALF_A], odd[HALF_A:]], axis=0)

    row4 = wide(jnp.stack([mine[0], by_low[0]], axis=2)[..., None])
    row5 = wide(
        jnp.stack([halves(by_high[0], mine[0]), halves(by_both[0], by_low[0])], axis=2)[..., None]
    )
    row6 = wide(mine[1][:, :, None, None])
    row7 = wide(halves(by_both[1], by_low[1])[:, :, None, None])
    columns = jnp.stack([row0, row1, row2, row3, row4, row5, row6, row7], axis=1)

    targets_first = (
        jnp.arange(2 * A0, dtype=jnp.int32)[:, None] * (NPTS // (2 * A0)) + checks_first
    ).reshape(A0, 2, R)
    targets_second = (
        jnp.arange(4 * A0, dtype=jnp.int32)[:, None] * (NPTS // (4 * A0)) + checks_second
    ).reshape(A0, 4, R)
    targets_third = (
        jnp.arange(8 * A0, dtype=jnp.int32)[:, None] * (NPTS // (8 * A0)) + checks_third
    ).reshape(A0, 4, 2 * R)
    ranks_mine = lax.dynamic_index_in_dim(ranks_third, box, 3, keepdims=False)
    rows, limits = [], []
    for side, groups in ((own, (group, group)), (other, (1 - group, group))):
        rows.append(
            jnp.concatenate(
                [by_parent(targets_first, 1, *groups), by_parent(targets_second, 1, *side)],
                axis=1,
            )
            * 4096
        )
        rows.append(by_parent(targets_third, 1, *side) * 4096)
        limit = by_parent(ranks_mine, 1, *side)
        limits += [jnp.broadcast_to(limit[:, t : t + 1], (A0, LANES)) for t in range(2)]
    return columns, jnp.stack(rows + limits, axis=1)


def per_device(
    coeffs,
    skeleton_first,
    skeleton_second,
    skeleton_third,
    checks_first,
    checks_second,
    checks_third,
    ranks_first,
    ranks_second,
    ranks_third,
    interpolants,
    owners,
):
    tbit = lax.axis_index("tbit")
    box = lax.axis_index("box")
    coeffs = coeffs[:, :, 0]

    def crossed(value, mask):
        return lax.ppermute(value, "tbit", [(k, k ^ mask) for k in range(4)])

    ranks = jnp.stack([ranks_first[:, :, 0], ranks_second[:, :, 0]])
    ranks = (ranks,) + tuple(crossed(ranks, mask) for mask in (1, 2, 3))
    even, odd = coeffs[:HALF_A, :, :, :LANES], coeffs[HALF_A:, :, :, :LANES]
    even, odd, ranks = lax.optimization_barrier((even, odd, ranks))
    near_even = crossed(even, 1)
    near_odd = crossed(odd, 3)
    columns, rows = tables(
        tbit, box, skeleton_first, skeleton_second, skeleton_third,
        checks_first, checks_second, checks_third, ranks, ranks_third,
    )
    high, low = build_operators(columns, rows, interpolants)
    slot_parent, slot_used = slot_table(
        lax.dynamic_index_in_dim(owners, tbit, 0, keepdims=False), 32, CAP
    )
    switched = exchange(
        coeffs, near_even, near_odd, high, low,
        slot_parent.reshape(-1), slot_used.reshape(-1).astype(jnp.int32),
    )
    return switched[None, None]


def solution(mesh):
    return jax.shard_map(
        per_device,
        mesh=mesh,
        in_specs=(
            P(None, "box", "tbit", None, None),
            P(None, "box", None, None),
            P(None, "box", None, None),
            P(None, "box", None, None),
            P(),
            P(),
            P(),
            P(None, "box", "tbit"),
            P(None, "box", "tbit"),
            P(),
            P(),
            P(),
        ),
        out_specs=P("tbit", "box", None, None, None, None, None),
        check_vma=False,
    )
```

```python
import functools

import jax
import jax.numpy as jnp
import numpy as np
from jax import lax
from jax.experimental import pallas as pl
from jax.experimental.pallas import tpu as pltpu
from jax.sharding import PartitionSpec as P

NPTS = 1048576
R = 64
A0 = 64
HALF_A = 32
LANES = 128
GROUP = 8
BATCH = 8
UNROLL = 4
CAP = 4
MESH = pl.DeviceIdType.MESH
f32 = jnp.float32
bf16 = jnp.bfloat16

SIN_COEFFS = (
    6.2831851600873945,
    -41.34165503088491,
    81.60100403766654,
    -76.54978142785076,
    39.53669915281796,
)

CHIP_STEPS = (
    (1, 0), (0, 1), (3, 0), (0, 3), (1, 1), (3, 3), (1, 3), (3, 1),
    (2, 1), (1, 2), (2, 3), (3, 2), (2, 0), (0, 2), (2, 2),
)

PIECES = ((0, 0, 32), (0, 32, 32), (1, 0, 64))


def split(value):
    high = value.astype(bf16)
    low = (value - high.astype(f32)).astype(bf16)
    return high, low


def dot(left, right):
    return jnp.dot(left, right, preferred_element_type=f32)


def dot3(left, right):
    return dot(left[0], right[0]) + dot(left[1], right[0]) + dot(left[0], right[1])


def cosines(scaled_rows, columns):
    phases = (scaled_rows * columns).astype(f32)
    turn = 0.25 - jnp.abs(phases) * (2.0**-32)
    square = turn * turn
    total = SIN_COEFFS[4]
    for coeff in SIN_COEFFS[3::-1]:
        total = total * square + coeff
    return total * turn


def operators_kernel(
    ranks, limits, first_ref, second_ref, third_ref, checks1, checks2, checks3, mats_ref,
    high_ref, low_ref, mats, mask4, mask2,
):
    step = pl.program_id(0)
    tbit = lax.axis_index("tbit")
    box = lax.axis_index("box")
    upper = step >= HALF_A // GROUP
    near = jnp.where(upper, tbit ^ 3, tbit ^ 1)
    other = jnp.where(upper, tbit ^ 1, tbit ^ 3)
    targets = (tbit, other)
    apart = ((0, 1), (jnp.where(upper, 0, 2), jnp.where(upper, 1, 3)))
    lane_block = lax.broadcasted_iota(jnp.int32, (1, 256), 1) // R

    def first_row(member):
        return jnp.concatenate(
            [
                first_ref[member, h, pl.ds(slot, 1), :]
                + (4 * (2 * box + h) + 2 * (slot % 2) + slot // 2) * (NPTS // 256)
                for h in range(2)
                for slot in (tbit, near)
            ],
            axis=1,
        )

    def second_row(member, target):
        slots = [tbit ^ distance for distance in apart[target]]
        return jnp.concatenate(
            [
                second_ref[member, h, pl.ds(slot, 1), :]
                + (2 * (2 * box + h) + slot % 2) * (NPTS // 128)
                for h in range(2)
                for slot in slots
            ],
            axis=1,
        )

    def third_row(member, target):
        return jnp.concatenate(
            [
                third_ref[member, h, pl.ds(targets[target], 1), :]
                + (2 * box + h) * (NPTS // 64)
                for h in range(2)
            ],
            axis=1,
        )

    def check_rows(member, target):
        a = step * GROUP + member
        i = targets[target]

        def points(ref, index, size):
            return (ref[pl.ds(index, 1), :] + index * size) * 4096

        x12 = [
            points(checks1, 2 * a + i // 2, NPTS // (2 * A0)),
            points(checks2, 4 * a + i, NPTS // (4 * A0)),
        ]
        x3 = [points(checks3, 8 * a + 2 * i + t, NPTS // (8 * A0)) for t in range(2)]
        return jnp.concatenate(x12, axis=1), jnp.concatenate(x3, axis=1)

    def rank_of(distance, level, member, h):
        return ranks[((distance * 2 + level) * A0 + step * GROUP + member) * 2 + h]

    def first_ranks(member, target):
        near0, near1 = apart[target]
        row = rank_of(near0, 0, member, 0)
        for block, (h, distance) in ((1, (0, near1)), (2, (1, near0)), (3, (1, near1))):
            row = jnp.where(lane_block == block, rank_of(distance, 0, member, h), row)
        return row

    def second_ranks(member, target):
        distance = (0, jnp.where(upper, 1, 3))[target]
        return jnp.where(
            lane_block < 2, rank_of(distance, 1, member, 0), rank_of(distance, 1, member, 1)
        )

    @pl.when(step == 0)
    def _():
        for level in range(3):
            high, low = split(mats_ref[level])
            mats[level] = jnp.concatenate([high, low, high, low], axis=1)
        row4 = lax.broadcasted_iota(jnp.int32, (256, 256), 0) // R
        col4 = lax.broadcasted_iota(jnp.int32, (256, 256), 1) // R
        mask4[...] = jnp.where(row4 == col4, 1.0, 0.0).astype(bf16)
        row2 = lax.broadcasted_iota(jnp.int32, (128, 256), 0) // R
        col2 = lax.broadcasted_iota(jnp.int32, (128, 256), 1) // LANES
        mask2[...] = jnp.where(row2 == col2, 1.0, 0.0).astype(bf16)

    rank_row = lax.broadcasted_iota(jnp.int32, (R, 256), 0)
    rank_half = lax.broadcasted_iota(jnp.int32, (R, LANES), 0)

    def doubled(kernel):
        high, low = split(kernel)
        return jnp.concatenate([high, high, low, low], axis=0)

    def masked(value, row):
        return split(jnp.where(rank_row < row, value, 0.0))

    def cut(value, member, target):
        first = ((step * GROUP + member) * 4 + targets[target]) * 2
        halves = [
            jnp.where(
                rank_half < limits[first + t],
                value[:, t * LANES : (t + 1) * LANES],
                0.0,
            )
            for t in range(2)
        ]
        return split(jnp.concatenate(halves, axis=0))

    def batch(units):
        points = []
        for member, target in units:
            x12, x3 = check_rows(member, target)
            x12 = jnp.broadcast_to(x12, (LANES, LANES)).T
            points.append(
                (jnp.concatenate([x12, x12], axis=1), jnp.broadcast_to(x3, (LANES, LANES)).T)
            )
        k1 = [
            doubled(cosines(p[0][:R], first_row(m))) for p, (m, t) in zip(points, units)
        ]
        first = [dot(mats[0], k) for k in k1]
        k2 = [
            doubled(cosines(p[0][R:], second_row(m, t)))
            for p, (m, t) in zip(points, units)
        ]
        second = [dot(mats[1], k) for k in k2]
        k3 = [
            cosines(p[1], third_row(m, t))
            for p, (m, t) in zip(points, units)
        ]
        k3 = [doubled(jnp.concatenate([k[:R], k[R:]], axis=1)) for k in k3]
        third = [dot(mats[2], k) for k in k3]
        first = [masked(v, first_ranks(m, t)) for v, (m, t) in zip(first, units)]
        blocks = [
            tuple(jnp.concatenate([part] * 4, axis=0) * mask4[...] for part in v) for v in first
        ]
        second = [masked(v, second_ranks(m, t)) for v, (m, t) in zip(second, units)]
        merged = [dot(jnp.concatenate(v, axis=0), b[0]) for v, b in zip(second, blocks)]
        extra = [dot(v[0], b[1]) for v, b in zip(second, blocks)]
        third = [cut(v, m, t) for v, (m, t) in zip(third, units)]
        merged = [split(v[:R] + v[R:] + e) for v, e in zip(merged, extra)]
        stacked = [
            tuple(jnp.concatenate([part] * 2, axis=0) * mask2[...] for part in v) for v in merged
        ]
        main = [
            dot(jnp.concatenate(v, axis=1), jnp.concatenate([b[0]] * 2, axis=0))
            for v, b in zip(third, stacked)
        ]
        rest = [dot(v[0], b[1]) for v, b in zip(third, stacked)]
        for v, e, (member, target) in zip(main, rest, units):
            high, low = split(v + e)
            high_ref[member, target] = high
            low_ref[member, target] = low

    units = [(m, t) for m in range(GROUP) for t in range(2)]
    for begin in range(0, len(units), BATCH):
        batch(units[begin : begin + BATCH])


def build_operators(ranks, limits, first, second, third, checks1, checks2, checks3, mats):
    shape = jax.ShapeDtypeStruct((A0, 2, LANES, 256), bf16)
    block = pl.BlockSpec((GROUP, 2, LANES, 256), lambda a: (a, 0, 0, 0))
    smem = pl.BlockSpec(memory_space=pltpu.SMEM)
    points = pl.BlockSpec((GROUP, 2, 4, R), lambda a: (a, 0, 0, 0))

    def whole(array):
        return pl.BlockSpec(array.shape, lambda a: (0,) * array.ndim)

    return pl.pallas_call(
        operators_kernel,
        grid=(A0 // GROUP,),
        out_shape=(shape, shape),
        in_specs=[smem, smem, points, points, points]
        + [whole(array) for array in (checks1, checks2, checks3, mats)],
        out_specs=(block, block),
        scratch_shapes=[
            pltpu.VMEM((3, R, 256), bf16),
            pltpu.VMEM((256, 256), bf16),
            pltpu.VMEM((LANES, 256), bf16),
        ],
        cost_estimate=pl.CostEstimate(
            flops=20_000_000_000, bytes_accessed=17_000_000, transcendentals=0
        ),
    )(ranks, limits, first, second, third, checks1, checks2, checks3, mats)


def peer_of(box, step):
    row = lax.rem(box // 8 + step // 8, 4)
    col = lax.rem((box // 2) % 4 + (step // 2) % 4, 4)
    core = lax.rem(box % 2 + step % 2, 2)
    return row * 8 + col * 2 + core


def exchange_kernel(
    coeffs, near_even, near_odd, high, low, parents, used, out,
    w_high, w_low, own, near_a, near_b, partial, *rest,
):
    count = len(PIECES)
    stages, sends, recvs = rest[:count], rest[count : 3 * count], rest[3 * count : 5 * count]
    (
        load_sem, own_sem, near_send, near_recv, part_send, part_recv,
        msg_send, msg_recv, self_sem,
    ) = rest[5 * count :]
    tbit = lax.axis_index("tbit")
    box = lax.axis_index("box")
    by_low = tbit + 1 - 2 * (tbit % 2)
    by_both = 3 - tbit

    def eight(group):
        return pl.ds(group * 8, 8)

    def load_operator(group):
        rows = eight(group)
        return (
            pltpu.make_async_copy(high.at[rows], w_high.at[rows], load_sem.at[0, group]),
            pltpu.make_async_copy(low.at[rows], w_low.at[rows], load_sem.at[1, group]),
        )

    def load_own(half, group):
        rows = eight(group)
        lanes = pl.ds(half * LANES, LANES)
        return pltpu.make_async_copy(
            coeffs.at[rows, :, :, lanes], own.at[rows], own_sem.at[half, group]
        )

    def load_near(group):
        side = near_even if group < 4 else near_odd
        return pltpu.make_async_copy(
            side.at[eight(group % 4)], near_a.at[eight(group)], load_sem.at[2, group]
        )

    for group in range(8):
        for copy in load_operator(group):
            copy.start()
        load_own(0, group).start()
        load_near(group).start()

    barrier = pltpu.get_barrier_semaphore()

    def greet(step, _):
        pl.semaphore_signal(
            barrier, inc=1, device_id=(tbit, peer_of(box, step)), device_id_type=MESH
        )
        return 0

    lax.fori_loop(1, 32, greet, 0)
    for side in (by_low, by_both):
        pl.semaphore_signal(barrier, inc=1, device_id=(side, box), device_id_type=MESH)
    pl.semaphore_wait(barrier, 33)

    def send_near(group):
        rows = eight(group)
        return pltpu.make_async_remote_copy(
            src_ref=coeffs.at[rows, :, :, pl.ds(LANES, LANES)],
            dst_ref=near_b.at[rows],
            send_sem=near_send.at[group],
            recv_sem=near_recv.at[group],
            device_id=(by_low if group < 4 else by_both, box),
            device_id_type=MESH,
        )

    def send_partial(half, piece, group):
        rows = eight(group)
        index = half * count + piece
        return pltpu.make_async_remote_copy(
            src_ref=sends[index].at[rows],
            dst_ref=recvs[index].at[rows],
            send_sem=part_send.at[index, group],
            recv_sem=part_recv.at[index, group],
            device_id=(by_both if group < 4 else by_low, box),
            device_id_type=MESH,
        )

    def multiply(half, near, group):
        def some(batch, _):
            members = [group * 8 + batch * UNROLL + k for k in range(UNROLL)]
            points = [
                split(jnp.concatenate([own[a, 0], near[a, 0], own[a, 1], near[a, 1]], axis=0))
                for a in members
            ]
            highs = [w_high[a].reshape(256, 256) for a in members]
            main = [
                dot(jnp.concatenate([h, w_low[a].reshape(256, 256)], axis=0), p[0])
                for h, a, p in zip(highs, members, points)
            ]
            extra = [dot(h, p[1]) for h, p in zip(highs, points)]
            for a, m, e in zip(members, main, extra):
                result = m[:256] + m[256:] + e
                partial[a] = result[:LANES].reshape(2, R, LANES)
                for piece, (t, begin, size) in enumerate(PIECES):
                    first = LANES + t * R + begin
                    sends[half * count + piece][a] = result[first : first + size]
            return 0

        lax.fori_loop(0, 8 // UNROLL, some, 0)

    def target(half, piece):
        t, begin, size = PIECES[piece]
        return out.at[t, :, box, pl.ds(begin, size), pl.ds(half * LANES, LANES)]

    def message(half, piece, step):
        index = half * count + piece
        return pltpu.make_async_remote_copy(
            src_ref=stages[piece].at[step],
            dst_ref=target(half, piece),
            send_sem=msg_send.at[index, step],
            recv_sem=msg_recv.at[index, step],
            device_id=(tbit, peer_of(box, step)),
            device_id_type=MESH,
        )

    def keep(half, piece):
        return pltpu.make_async_copy(
            stages[piece].at[0], target(half, piece), self_sem.at[half, piece]
        )

    def fill(half, piece, step):
        t, begin, size = PIECES[piece]
        owner = peer_of(box, step)
        for slot in range(CAP):
            parent = parents[owner * CAP + slot]
            live = used[owner * CAP + slot]
            value = partial[parent, t, begin : begin + size]
            value = value + recvs[half * count + piece][parent]
            stages[piece][step, slot] = jnp.where(jnp.full((size, LANES), live) > 0, value, 0.0)

    def release(half, piece):
        for group in range(8):
            send_partial(half, piece, group).wait_recv()
        if half == 1:
            keep(0, piece).wait()

        def go(step):
            if half == 1:
                message(0, piece, step).wait_send()
            fill(half, piece, step)
            message(half, piece, step).start()

        go(1)
        for core in range(2):
            for row, col in CHIP_STEPS:
                go(row * 8 + col * 2 + core)
        fill(half, piece, 0)
        keep(half, piece).start()

    for group in range(8):
        for copy in load_operator(group):
            copy.wait()
        load_own(0, group).wait()
        load_near(group).wait()
        multiply(0, near_a, group)
        load_own(1, group).start()
        send_partial(0, 0, group).start()
    for piece in range(1, count):
        for group in range(8):
            send_partial(0, piece, group).start()
    for group in range(8):
        send_near(group).start()
    for piece in range(count):
        release(0, piece)

    for group in range(8):
        load_own(1, group).wait()
        send_near(group).wait_recv()
        multiply(1, near_b, group)
        send_partial(1, 0, group).start()
    for piece in range(1, count):
        for group in range(8):
            send_partial(1, piece, group).start()
    for piece in range(count):
        release(1, piece)

    for piece in range(count):
        keep(1, piece).wait()

        def finish(step, _):
            message(1, piece, step).wait_send()
            message(0, piece, step).wait_recv()
            message(1, piece, step).wait_recv()
            return 0

        lax.fori_loop(1, 32, finish, 0)
    for group in range(8):
        send_near(group).wait_send()
        for half in range(2):
            for piece in range(count):
                send_partial(half, piece, group).wait_send()


def exchange(coeffs, near_even, near_odd, high, low, parents, used):
    hbm = pl.BlockSpec(memory_space=pl.ANY)
    smem = pl.BlockSpec(memory_space=pltpu.SMEM)
    count = len(PIECES)
    parts = [pltpu.VMEM((A0, size, LANES), f32) for _, _, size in PIECES]
    halves = pltpu.VMEM((A0, 2, R, LANES), f32)
    dma = pltpu.SemaphoreType.DMA
    return pl.pallas_call(
        exchange_kernel,
        out_shape=jax.ShapeDtypeStruct((2, CAP, 32, R, 256), f32),
        in_specs=[hbm] * 5 + [smem] * 2,
        out_specs=hbm,
        scratch_shapes=[
            pltpu.VMEM((A0, 2, LANES, 256), bf16),
            pltpu.VMEM((A0, 2, LANES, 256), bf16),
            halves, halves, halves, halves,
        ]
        + [pltpu.VMEM((32, CAP, size, LANES), f32) for _, _, size in PIECES]
        + parts * 4
        + [
            dma((3, 8)), dma((2, 8)), dma((8,)), dma((8,)),
            dma((2 * count, 8)), dma((2 * count, 8)),
            dma((2 * count, 32)), dma((2 * count, 32)), dma((2, count)),
        ],
        compiler_params=pltpu.CompilerParams(
            collective_id=0, has_side_effects=True, vmem_limit_bytes=62 << 20
        ),
    )(coeffs, near_even, near_odd, high, low, parents, used)


def slot_table(owner_row, box_count, capacity):
    parent_count = owner_row.shape[0]
    onehot = (owner_row[:, None] == jnp.arange(box_count, dtype=jnp.int32)[None, :]).astype(
        jnp.int32
    )
    earlier = jnp.cumsum(onehot, axis=0, dtype=jnp.int32) - onehot
    slot_of = jnp.sum(earlier * onehot, axis=1, dtype=jnp.int32)
    matches = (onehot.T[:, None, :] == 1) & (
        slot_of[None, None, :] == jnp.arange(capacity, dtype=jnp.int32)[None, :, None]
    )
    slot_parent = jnp.sum(
        jnp.where(matches, jnp.arange(parent_count, dtype=jnp.int32)[None, None, :], 0), axis=2
    )
    slot_used = jnp.any(matches, axis=2)
    return (slot_parent, slot_used)


def per_device(
    coeffs,
    skeleton_first,
    skeleton_second,
    skeleton_third,
    checks_first,
    checks_second,
    checks_third,
    ranks_first,
    ranks_second,
    ranks_third,
    interpolants,
    owners,
):
    tbit = lax.axis_index("tbit")
    box = lax.axis_index("box")
    coeffs = coeffs[:, :, 0]

    def crossed(value, mask):
        return lax.ppermute(value, "tbit", [(k, k ^ mask) for k in range(4)])

    ranks = jnp.stack([ranks_first[:, :, 0], ranks_second[:, :, 0]])
    ranks = (ranks,) + tuple(crossed(ranks, mask) for mask in (1, 2, 3))
    even, odd = coeffs[:HALF_A, :, :, :LANES], coeffs[HALF_A:, :, :, :LANES]
    even, odd, ranks = lax.optimization_barrier((even, odd, ranks))
    near_even = crossed(even, 1)
    near_odd = crossed(odd, 3)
    limits = lax.dynamic_index_in_dim(ranks_third, box, 3, keepdims=False)
    high, low = build_operators(
        jnp.stack(ranks).reshape(-1), limits.reshape(-1),
        skeleton_first, skeleton_second, skeleton_third,
        checks_first, checks_second, checks_third, interpolants,
    )
    slot_parent, slot_used = slot_table(
        lax.dynamic_index_in_dim(owners, tbit, 0, keepdims=False), 32, CAP
    )
    switched = exchange(
        coeffs, near_even, near_odd, high, low,
        slot_parent.reshape(-1), slot_used.reshape(-1).astype(jnp.int32),
    )
    return switched[None, None]


def solution(mesh):
    return jax.shard_map(
        per_device,
        mesh=mesh,
        in_specs=(
            P(None, "box", "tbit", None, None),
            P(None, "box", None, None),
            P(None, "box", None, None),
            P(None, "box", None, None),
            P(),
            P(),
            P(),
            P(None, "box", "tbit"),
            P(None, "box", "tbit"),
            P(),
            P(),
            P(),
        ),
        out_specs=P("tbit", "box", None, None, None, None, None),
        check_vma=False,
    )
```
